32 devices in a mesh: dp: 8 (over y, x, core), tensor: 4 (over z).
Axes of the slice: x: 2, y: 2, z: 4, core: 2. Of those that a mesh axis runs over, the one named last changes fastest.
Arguments:
- layer_input: bfloat16 [16384, 768], P(('dp', 'tensor')), may hold values from -3.7 to 3.7
- w_qkv: bfloat16 [768, 3, 768], P(None, None, 'tensor'), may hold values from -0.3125 to 0.3125
- b_qv: bfloat16 [2, 768], P(None, 'tensor'), may hold values from -3 to 3
- w_out: bfloat16 [768, 768], P('tensor'), may hold values from -0.21875 to 0.21875
- b_out: bfloat16 [768], replicated, may hold values from -1.75 to 1.75
- conv_w: bfloat16 [12, 33], P('tensor'), may hold values from -1.25 to 1.25
- norm1_gain: bfloat16 [768], replicated, may hold values from 0.5 to 1.5
- norm1_bias: bfloat16 [768], replicated, may hold values from -1.75 to 1.75
- w_in: bfloat16 [768, 3072], P(None, 'tensor'), may hold values from -0.21875 to 0.21875
- b_in: bfloat16 [3072], P('tensor'), may hold values from -1.75 to 1.75
- w_back: bfloat16 [3072, 768], P('tensor'), may hold values from -0.109375 to 0.109375
- b_back: bfloat16 [768], replicated, may hold values from -1.75 to 1.75
- norm2_gain: bfloat16 [768], replicated, may hold values from 0.5 to 1.5
- norm2_bias: bfloat16 [768], replicated, may hold values from -1.75 to 1.75
- output_grad: bfloat16 [16384, 768], P(('dp', 'tensor')), may hold values from -6 to 6
- item_length: int32 [10], replicated, may hold values from 512 to 2048, as said below
- item_group: int32 [10], replicated, may hold values from 0 to 7, as said below
- item_offset: int32 [10], replicated, may hold values from 0 to 1536, as said below
Outputs:
- output: float32 [16384, 768], P(('dp', 'tensor'))
- input_grad: float32 [16384, 768], P(('dp', 'tensor'))
- w_qkv_grad: float32 [768, 3, 768], P(None, None, 'tensor')
- b_qv_grad: float32 [2, 768], P(None, 'tensor')
- w_out_grad: float32 [768, 768], P('tensor')
- b_out_grad: float32 [768], replicated
- conv_w_grad: float32 [12, 33], P('tensor')
- norm1_gain_grad: float32 [768], replicated
- norm1_bias_grad: float32 [768], replicated
- w_in_grad: float32 [768, 3072], P(None, 'tensor')
- b_in_grad: float32 [3072], P('tensor')
- w_back_grad: float32 [3072, 768], P('tensor')
- b_back_grad: float32 [768], replicated
- norm2_gain_grad: float32 [768], replicated
- norm2_bias_grad: float32 [768], replicated
The draws below stay inside these ranges and needn't reach their ends.
Inputs may be any that keep to these rules, and one draw needn't show every extreme that they name: `item_length`: each item has 512 or 2048 tokens; 4 items have 2048. `item_group`: every group holds either one item of 2048 tokens or one or two items of 512; some hold two. `item_offset`: A multiple of 512; items of one group never intersect; rows of a group that no item covers are padding.
All inputs are finite; a program needn't handle non-finite values.
Results may differ from the reference program's by a relative error of at most 0.018.
Values may be sent and summed in bfloat16 or wider, within the bound.
No kernel may reach another device: no remote copies, remote signals or barrier semaphores. Data moves between devices by JAX's collectives and lax.ppermute only.
A program may use at most 256 MiB of HBM per device.

```python
import math
import jax
import jax.numpy as jnp
from jax import lax

D = 768
HEADS = 12
FF = 3072
LAND = 64
NS_STEPS = 6
KSIZE = 33
LONG = 2048
SHORT = 512
ITEMS = 10
TOKENS = 16384
N_DP = 8


def item_table(key):
    base = jax.random.fold_in(key, 7)
    first_key, second_key, third_key, fourth_key = jax.random.split(base, 4)
    half_groups = N_DP // 2
    quarter_groups = N_DP // 4
    order = jax.random.permutation(first_key, N_DP).astype(jnp.int32)
    long_group = order[:half_groups]
    short_index = jnp.arange(3 * quarter_groups, dtype=jnp.int32)
    paired = short_index < 2 * quarter_groups
    pair_index = jnp.minimum(short_index // 2, quarter_groups - 1)
    single_index = jnp.clip(short_index - 2 * quarter_groups, 0, quarter_groups - 1)
    short_group = jnp.where(paired, order[half_groups + pair_index], order[half_groups + quarter_groups + single_index])
    first_slot = jax.random.randint(second_key, (quarter_groups,), 0, 4, dtype=jnp.int32)
    second_slot = (first_slot + jax.random.randint(third_key, (quarter_groups,), 1, 4, dtype=jnp.int32)) % 4
    single_slot = jax.random.randint(fourth_key, (quarter_groups,), 0, 4, dtype=jnp.int32)
    single_slot = single_slot.at[0].set(3)
    pair_slot = jnp.where(short_index % 2 == 0, first_slot[pair_index], second_slot[pair_index])
    short_slot = jnp.where(paired, pair_slot, single_slot[single_index])
    lengths = jnp.concatenate([jnp.full((half_groups,), LONG, jnp.int32), jnp.full((3 * quarter_groups,), SHORT, jnp.int32)])
    groups = jnp.concatenate([long_group, short_group])
    offsets = jnp.concatenate([jnp.zeros((half_groups,), jnp.int32), short_slot * SHORT])
    shuffle = jax.random.permutation(jax.random.fold_in(base, 11), ITEMS)
    return (lengths[shuffle], groups[shuffle], offsets[shuffle])


def draw_item_length(key, part):
    return item_table(key)[0]


def draw_item_group(key, part):
    return item_table(key)[1]


def draw_item_offset(key, part):
    return item_table(key)[2]


def draw_layer_input(key, part):
    first_key, second_key, third_key = jax.random.split(jax.random.fold_in(key, 3), 3)
    positions = (jnp.arange(TOKENS, dtype=jnp.int32) % LONG).astype(jnp.float32)
    freqs = jnp.exp(jax.random.uniform(second_key, (D,), jnp.float32, math.log(2.0 * math.pi / 1024.0), math.log(2.0 * math.pi / 64.0)))
    phases = jax.random.uniform(third_key, (TOKENS // LONG, D), jnp.float32, -math.pi, math.pi)
    phase_rows = jnp.repeat(phases, LONG, axis=0)
    waves = jnp.cos(positions[:, None] * freqs[None, :] + phase_rows)
    rough = jax.random.truncated_normal(first_key, -4.0, 4.0, (TOKENS, D), jnp.float32)
    amplitude = 0.9
    return (0.7 * rough + amplitude * waves).astype(jnp.bfloat16)


def steps_of(stream_key, extent, cuts, least, top_value):
    loudness = 1.0
    for dim, shards_of in cuts:
        draws = jax.random.uniform(jax.random.fold_in(jax.random.fold_in(stream_key, 6), dim), (shards_of,), jnp.float32, least / len(cuts), top_value / len(cuts))
        loudness = loudness * jnp.repeat(jnp.exp(draws), extent[dim] // shards_of).reshape((-1,) + (1,) * (len(extent) - 1 - dim))
    return loudness


def centred(stream_key, extent, deviation, limit, shards=(), held_as=jnp.bfloat16):
    entries = deviation * jax.random.normal(stream_key, extent, jnp.float32)
    if shards:
        entries = entries * steps_of(stream_key, extent, shards, -0.22, 0.18)
    return jnp.clip(entries, -limit, limit).astype(held_as)


def setup_inputs(seed: int = 0) -> dict:
    seeds = jax.random.split(jax.random.key(seed), 19)
    layer_input = draw_layer_input(jax.random.fold_in(seeds[18], 71), 0)
    w_qkv = centred(seeds[1], (D, 3, D), (D // 2) ** -0.5, 0.3125, ((2, 4),))
    b_qv = centred(seeds[2], (2, D), 0.5, 3.0, ((1, 4),))
    w_out = centred(seeds[3], (D, D), D ** -0.5, 0.21875, ((0, 4),))
    b_out = centred(seeds[4], (D,), 0.3, 1.75)
    conv_w = centred(seeds[5], (HEADS, KSIZE), 0.2, 1.25, ((0, 4),))
    norm1_gain = jnp.clip(1.0 + 0.1 * jax.random.normal(seeds[6], (D,), jnp.float32), 0.5, 1.5).astype(jnp.bfloat16)
    norm1_bias = centred(seeds[7], (D,), 0.3, 1.75)
    w_in = centred(seeds[8], (D, FF), D ** -0.5, 0.21875, ((1, 4),))
    b_in = centred(seeds[9], (FF,), 0.3, 1.75, ((0, 4),))
    w_back = centred(seeds[10], (FF, D), FF ** -0.5, 0.109375, ((0, 4),))
    b_back = centred(seeds[11], (D,), 0.3, 1.75)
    norm2_gain = jnp.clip(1.0 + 0.1 * jax.random.normal(seeds[12], (D,), jnp.float32), 0.5, 1.5).astype(jnp.bfloat16)
    norm2_bias = centred(seeds[13], (D,), 0.3, 1.75)
    output_grad = centred(seeds[14], (TOKENS, D), 1.0, 6.0, ((0, 32),))
    item_length = draw_item_length(jax.random.fold_in(seeds[18], 71), 0)
    item_group = draw_item_group(jax.random.fold_in(seeds[18], 71), 0)
    item_offset = draw_item_offset(jax.random.fold_in(seeds[18], 71), 0)
    return {"layer_input": layer_input, "w_qkv": w_qkv, "b_qv": b_qv, "w_out": w_out, "b_out": b_out, "conv_w": conv_w, "norm1_gain": norm1_gain, "norm1_bias": norm1_bias, "w_in": w_in, "b_in": b_in, "w_back": w_back, "b_back": b_back, "norm2_gain": norm2_gain, "norm2_bias": norm2_bias, "output_grad": output_grad, "item_length": item_length, "item_group": item_group, "item_offset": item_offset}


highest = lax.Precision.HIGHEST
eps = 1e-05
big_negative = -1e+30

@jax.custom_vjp
def low(v):
    return lax.optimization_barrier(v.astype(jnp.bfloat16)).astype(jnp.float32)

@jax.custom_vjp
def low_back(v):
    return v

def low_keep(v):
    return (low(v), None)

def low_pass(kept, grad):
    return (grad,)

def back_keep(v):
    return (v, None)

def back_low(kept, grad):
    return (low(grad),)
low.defvjp(low_keep, low_pass)
low_back.defvjp(back_keep, back_low)

def both_ways(value):
    return low(low_back(value))

def exact_gelu(value):
    return jax.nn.gelu(value, approximate=False)

def layout(item_length, item_group, item_offset, group_index, row_count):
    positions = jnp.arange(row_count, dtype=jnp.int32)
    first_row = item_offset[:, None]
    item_size = item_length[:, None]
    member = (item_group[:, None] == group_index) & (positions[None, :] >= first_row) & (positions[None, :] < first_row + item_size)
    live = jnp.any(member, axis=0)
    row_start = lax.optimization_barrier(jnp.sum(jnp.where(member, first_row, 0), axis=0, dtype=jnp.int32))
    row_size = jnp.maximum(lax.optimization_barrier(jnp.sum(jnp.where(member, item_size, 0), axis=0, dtype=jnp.int32)), 1)
    row_slot = jnp.where(live, row_start // SHORT, -1)
    row_col = jnp.where(live, row_slot * LAND + (positions - row_start) * LAND // row_size, -1)
    return (live, row_slot, row_col)

def landmark_inverse(query_land, key_land, scale):
    scores = jnp.einsum('slhd,smhd->shlm', query_land, key_land, precision=highest) * scale
    weight = jax.nn.softmax(scores, axis=-1)
    row_top = lax.optimization_barrier(jnp.max(lax.optimization_barrier(jnp.sum(weight, axis=-1)), axis=-1))
    col_top = lax.optimization_barrier(jnp.max(lax.optimization_barrier(jnp.sum(weight, axis=-2)), axis=-1))
    inverse = jnp.swapaxes(weight, -1, -2) / (row_top * col_top)[:, :, None, None]
    identity = jnp.eye(weight.shape[-1], dtype=jnp.float32)
    for sweep_index in range(NS_STEPS):
        product = jnp.matmul(weight, inverse, precision=highest)
        factor = 7.0 * identity - product
        factor = 15.0 * identity - jnp.matmul(product, factor, precision=highest)
        factor = 13.0 * identity - jnp.matmul(product, factor, precision=highest)
        inverse = 0.25 * jnp.matmul(inverse, factor, precision=highest)
    return inverse

def depthwise(values, kernel, row_slot):
    reach = kernel.shape[1] // 2
    row_count = values.shape[0]
    padded = jnp.pad(values, ((reach, reach), (0, 0), (0, 0)))
    slot_padded = jnp.pad(row_slot, (reach, reach), constant_values=-1)
    result = jnp.zeros_like(values)
    for offset in range(kernel.shape[1]):
        same_item = (slot_padded[offset:offset + row_count] == row_slot) & (row_slot >= 0)
        result = result + jnp.where(same_item[:, None, None], padded[offset:offset + row_count], 0.0) * kernel[:, offset][None, :, None]
    return result

def normalize(summed, gain, shift):
    centered = summed - lax.optimization_barrier(jnp.mean(summed, axis=-1, keepdims=True))
    spread = lax.optimization_barrier(jnp.mean(centered * centered, axis=-1, keepdims=True))
    return centered * lax.rsqrt(spread + eps) * gain + shift

def attention_block(query, keys, values, kernel, live, row_slot, row_col):
    row_count = query.shape[0]
    heads = query.shape[1]
    head_size = query.shape[2]
    columns = row_count // SHORT * LAND
    slot_count = columns // LAND
    scale = 1.0 / math.sqrt(head_size)
    column_ids = jnp.arange(columns, dtype=jnp.int32)
    picker = (row_col[None, :] == column_ids[:, None]).astype(jnp.float32)
    per_column = jnp.maximum(lax.optimization_barrier(jnp.sum(picker, axis=1)), 1.0)
    allowed = row_slot[:, None] == (column_ids // LAND)[None, :]
    live_wide = live.astype(jnp.float32)
    query_land = both_ways(jnp.einsum('cr,rhd->chd', picker, query, precision=highest) / per_column[:, None, None])
    key_land = both_ways(jnp.einsum('cr,rhd->chd', picker, keys, precision=highest) / per_column[:, None, None])
    scores_f = low_back(jnp.einsum('rhd,chd->hrc', query, key_land, precision=highest) * scale)
    f_mat = both_ways(jax.nn.softmax(jnp.where(allowed[None], scores_f, big_negative), axis=-1) * live_wide[None, :, None])
    inverse = landmark_inverse(query_land.reshape(slot_count, LAND, heads, head_size), key_land.reshape(slot_count, LAND, heads, head_size), scale)
    scores_b = low_back(jnp.einsum('chd,rhd->hcr', query_land, keys, precision=highest) * scale)
    b_mat = both_ways(jax.nn.softmax(jnp.where(jnp.transpose(allowed)[None], scores_b, big_negative), axis=-1))
    carried = low_back(jnp.einsum('hcr,rhd->chd', b_mat, values, precision=highest))
    mixed = both_ways(jnp.einsum('shlm,smhd->slhd', inverse, carried.reshape(slot_count, LAND, heads, head_size), precision=highest).reshape(columns, heads, head_size))
    attention = jnp.einsum('hrc,chd->rhd', f_mat, mixed, precision=highest)
    return both_ways((attention + depthwise(values, kernel, row_slot)).reshape(row_count, heads * head_size))

def layer(params, tokens, live, row_slot, row_col):
    w_qkv, b_qv, w_out, b_out, kernel, gain_one, shift_one, w_in, b_in, w_back, b_back, gain_two, shift_two = params
    row_count = tokens.shape[0]
    heads = kernel.shape[0]
    head_size = w_qkv.shape[2] // heads
    projected = jnp.einsum('rd,dke->rke', tokens, w_qkv, precision=highest)
    query = both_ways(projected[:, 0] + b_qv[0]).reshape(row_count, heads, head_size)
    keys = both_ways(projected[:, 1]).reshape(row_count, heads, head_size)
    values = both_ways(projected[:, 2] + b_qv[1]).reshape(row_count, heads, head_size)
    attended = attention_block(query, keys, values, kernel, live, row_slot, row_col)
    summed_one = tokens + low_back(jnp.dot(attended, w_out, precision=highest)) + b_out
    normed = normalize(summed_one, gain_one, shift_one)
    pre_act = low_back(jnp.dot(low(normed), w_in, precision=highest) + b_in)
    hidden = low(exact_gelu(pre_act))
    summed_two = normed + low_back(jnp.dot(hidden, w_back, precision=highest)) + b_back
    return normalize(summed_two, gain_two, shift_two)

def reference(layer_input, w_qkv, b_qv, w_out, b_out, conv_w, norm1_gain, norm1_bias, w_in, b_in, w_back, b_back, norm2_gain, norm2_bias, output_grad, item_length, item_group, item_offset):
    params = tuple((weight.astype(jnp.float32) for weight in (w_qkv, b_qv, w_out, b_out, conv_w, norm1_gain, norm1_bias, w_in, b_in, w_back, b_back, norm2_gain, norm2_bias)))
    group_ids = jnp.arange(N_DP, dtype=jnp.int32)
    live, row_slot, row_col = jax.vmap(lambda group_index: layout(item_length, item_group, item_offset, group_index, LONG))(group_ids)
    grouped = layer_input.astype(jnp.float32).reshape(N_DP, LONG, D)

    def forward(weights, tokens):

        def one_group(carry, pieces):
            return (carry, layer(weights, pieces[0], pieces[1], pieces[2], pieces[3]))
        unused, results = lax.scan(jax.checkpoint(one_group), jnp.zeros((), jnp.float32), (tokens, live, row_slot, row_col))
        return results
    output, pullback = jax.vjp(forward, params, grouped)
    weight_grads, input_grad = pullback(output_grad.astype(jnp.float32).reshape(N_DP, LONG, D))
    return (output.reshape(TOKENS, D), input_grad.reshape(TOKENS, D), weight_grads[0], weight_grads[1], weight_grads[2], weight_grads[3], weight_grads[4], weight_grads[5], weight_grads[6], weight_grads[7], weight_grads[8], weight_grads[9], weight_grads[10], weight_grads[11], weight_grads[12])
```

```python
from functools import partial
import math

import jax
import jax.numpy as jnp
import numpy as np
from jax import lax
from jax.sharding import PartitionSpec as P

LAND = 64
NS_STEPS = 6
SHORT = 512
REACH = 16

highest = lax.Precision.HIGHEST
eps = 1e-05
f32 = jnp.float32
bf16 = jnp.bfloat16


def dot(left, right, dims, precision=None):
    return lax.dot_general(
        left, right, (dims, ((), ())), preferred_element_type=f32, precision=precision
    )


def nn(left, right):
    return dot(left, right, ((1,), (0,)))


def nt(left, right):
    return dot(left, right, ((1,), (1,)))


def tn(left, right):
    return dot(left, right, ((0,), (0,)))


def landmark_inverse(query_land, key_land, scale):
    scores = jnp.einsum("lhd,mhd->hlm", query_land, key_land, precision=highest) * scale
    weight = jax.nn.softmax(scores, axis=-1)
    row_top = jnp.max(jnp.sum(weight, axis=-1), axis=-1)
    col_top = jnp.max(jnp.sum(weight, axis=-2), axis=-1)
    inverse = jnp.swapaxes(weight, -1, -2) / (row_top * col_top)[:, None, None]
    identity = jnp.eye(weight.shape[-1], dtype=f32)
    for sweep_index in range(NS_STEPS):
        product = jnp.matmul(weight, inverse, precision=highest)
        factor = 7.0 * identity - product
        factor = 15.0 * identity - jnp.matmul(product, factor, precision=highest)
        factor = 13.0 * identity - jnp.matmul(product, factor, precision=highest)
        inverse = 0.25 * jnp.matmul(inverse, factor, precision=highest)
    return inverse


def normalize(summed, gain, shift):
    centered = summed - jnp.mean(summed, axis=-1, keepdims=True)
    spread = jnp.mean(centered * centered, axis=-1, keepdims=True)
    return centered * lax.rsqrt(spread + eps) * gain + shift


def norm_forward(summed, gain, shift):
    centered = summed - jnp.mean(summed, axis=-1, keepdims=True)
    spread = jnp.mean(centered * centered, axis=-1, keepdims=True)
    inv = lax.rsqrt(spread + eps)
    unit = centered * inv
    return unit * gain + shift, unit, inv


def norm_backward(grad, unit, inv, gain):
    scaled = grad * gain
    first = jnp.mean(scaled, axis=-1, keepdims=True)
    second = jnp.mean(scaled * unit, axis=-1, keepdims=True)
    return inv * (scaled - first - unit * second)


def banded(kernel, block):
    heads, taps = kernel.shape
    wide = block + taps - 1
    padded = jnp.pad(kernel, ((0, 0), (0, wide + 1 - taps)))
    tiled = jnp.tile(padded, (1, block))[:, : block * wide]
    return tiled.reshape(heads, block, wide)


def on_device(
    dp_size,
    tp_size,
    layer_input,
    w_qkv,
    b_qv,
    w_out,
    b_out,
    conv_w,
    norm1_gain,
    norm1_bias,
    w_in,
    b_in,
    w_back,
    b_back,
    norm2_gain,
    norm2_bias,
    output_grad,
    item_length,
    item_group,
    item_offset,
):
    rows, width = layer_input.shape
    local_width = w_qkv.shape[2]
    local_heads = conv_w.shape[0]
    head_size = local_width // local_heads
    heads = local_heads * tp_size
    scale = 1.0 / math.sqrt(head_size)
    dp_at = lax.axis_index("dp")
    tp_at = lax.axis_index("tensor")
    sizes = {"dp": dp_size, "tensor": tp_size}
    places = {"dp": dp_at, "tensor": tp_at}
    dp_bits = dp_size.bit_length() - 1
    tp_bits = tp_size.bit_length() - 1
    on_tensor = [("tensor", bit) for bit in range(tp_bits)]
    on_core = [("dp", 0)]
    up = [("dp", bit) for bit in range(1, dp_bits)]
    down = up[::-1]
    axes = on_core + down + on_tensor[::-1]

    def partner(value, step, distance=None):
        axis, bit = step
        flip = distance if distance is not None else 1 << bit
        return lax.ppermute(value, axis, [(at, at ^ flip) for at in range(sizes[axis])])

    def is_upper(step):
        return (places[step[0]] >> step[1]) & 1

    def joined(value, other, upper, axis):
        if upper is None:
            return jnp.concatenate([value, other], axis=axis)
        first = jnp.where(upper == 1, other, value)
        second = jnp.where(upper == 1, value, other)
        return jnp.concatenate([first, second], axis=axis)

    def gather_steps(mine, steps, order, absolute):
        held = mine.reshape((1,) * len(order) + mine.shape)
        for step in steps:
            other = partner(held, step)
            held = joined(held, other, is_upper(step) if absolute else None, order.index(step))
        return held.reshape((-1,) + mine.shape[1:])

    def own_share(local):
        share = local.shape[0] // dp_size
        return lax.dynamic_slice_in_dim(local, dp_at * share, share, axis=0)

    plain = on_tensor[::-1] + down + on_core

    def gather_plain(local, middle):
        return gather_steps(own_share(local), on_tensor[::-1] + middle + on_core, plain, True)

    def gather_near(local, middle):
        return gather_steps(own_share(local), on_tensor[::-1] + middle + on_core, axes, False)

    def scatter_plain(partial_sum, middle):
        held = partial_sum.reshape((2,) * len(plain) + (-1, partial_sum.shape[1]))
        left = list(plain)
        for step in on_core + middle + on_tensor:
            at = left.index(step)
            upper = is_upper(step)
            sent = lax.dynamic_index_in_dim(held, 1 - upper, axis=at, keepdims=False)
            kept = lax.dynamic_index_in_dim(held, upper, axis=at, keepdims=False)
            held = kept + partner(sent.astype(bf16), step).astype(f32)
            left.remove(step)
        return held

    def scatter_near(partial_sum, middle):
        held = partial_sum.reshape((2,) * len(axes) + (-1, partial_sum.shape[1]))
        left = list(axes)
        for step in on_core + middle + on_tensor:
            at = left.index(step)
            sent = lax.index_in_dim(held, 1, axis=at, keepdims=False)
            kept = lax.index_in_dim(held, 0, axis=at, keepdims=False)
            held = kept + partner(sent.astype(bf16), step).astype(f32)
            left.remove(step)
        return held

    def over_tensor(value):
        parts = [value] + [partner(value, ("tensor", 0), far) for far in range(1, tp_size)]
        for bit in range(tp_bits):
            upper = is_upper(("tensor", bit)) == 1
            parts = [jnp.where(upper, parts[at ^ (1 << bit)], parts[at]) for at in range(tp_size)]
        return jnp.stack(parts)

    def sum_tensor(value):
        parts = [value] + [partner(value, ("tensor", 0), far) for far in range(1, tp_size)]
        while len(parts) > 1:
            parts = [parts[at] + parts[at + 1] for at in range(0, len(parts), 2)]
        return parts[0]

    def over_dp(piece, middle):
        return gather_steps(piece, middle + on_core, down + on_core, True)

    local_qkv = jnp.transpose(w_qkv, (1, 2, 0)).reshape(3 * local_width, width)
    full_q = gather_plain(local_qkv[:local_width], up)
    full_k = gather_plain(local_qkv[local_width : 2 * local_width], up)
    full_v = gather_plain(local_qkv[2 * local_width :], down)
    full_out = gather_plain(w_out, down)
    full_in = gather_near(jnp.transpose(w_in), up)
    full_back = gather_near(w_back, down)
    small = jnp.concatenate(
        [
            b_qv.astype(f32).reshape(2, local_width),
            jnp.pad(conv_w.astype(f32).reshape(1, -1), ((0, 0), (0, local_width - conv_w.size))),
            b_in.astype(f32).reshape(-1, local_width),
        ]
    )
    small_all = over_tensor(small)
    bias_q = small_all[:, 0].reshape(-1)
    bias_v = small_all[:, 1].reshape(-1)
    conv_all = small_all[:, 2, : conv_w.size].reshape(heads, conv_w.shape[1])
    hidden_share = b_in.shape[0] // dp_size
    bias_plain = small_all[:, 3:].reshape(dp_size * tp_size, hidden_share)
    codes = jnp.zeros((), jnp.int32)
    plain_index = np.zeros((1,), np.int32)
    for step in axes:
        weight = (1 << step[1]) * (dp_size if step[0] == "tensor" else 1)
        codes = codes + is_upper(step) * weight
        plain_index = (plain_index[:, None] + np.array([0, weight], np.int32)).reshape(-1)
    near_to_plain = plain_index ^ codes
    plain_to_near = jnp.asarray(np.argsort(plain_index).astype(np.int32))[jnp.arange(dp_size * tp_size) ^ codes]
    bias_in = bias_plain[near_to_plain].reshape(-1)

    first_row = tp_at * rows
    holds = (
        (item_group == dp_at)
        & (item_offset <= first_row)
        & (first_row < item_offset + item_length)
    )
    live = jnp.any(holds)
    size = jnp.sum(jnp.where(holds, item_length, 0))
    is_long = size > SHORT
    live_f = live.astype(f32)
    row_ids = jnp.arange(rows, dtype=jnp.int32)
    land_ids = jnp.arange(LAND, dtype=jnp.int32)
    share_long = LAND // tp_size
    per_short = rows // LAND
    per_long = rows // share_long
    per_column = jnp.where(is_long, per_long, per_short).astype(f32)
    pick_short = ((row_ids // per_short)[None, :] == land_ids[:, None]).astype(bf16)
    pick_long = (
        (row_ids // per_long)[None, :] == jnp.arange(share_long, dtype=jnp.int32)[:, None]
    ).astype(bf16)

    query = (nt(layer_input, full_q) + bias_q).astype(bf16)
    keys = nt(layer_input, full_k).astype(bf16)
    values = (nt(layer_input, full_v) + bias_v).astype(bf16)

    both = jnp.concatenate([query, keys], axis=1)
    land_short = (nn(pick_short, both) / per_short).astype(bf16)
    land_long = (nn(pick_long, both) / per_long).astype(bf16)
    land_all = jnp.where(is_long, over_tensor(land_long).reshape(LAND, 2 * width), land_short)
    query_land = land_all[:, :width]
    key_land = land_all[:, width:]

    def halo(value):
        along = [(at, at + 1) for at in range(tp_size - 1)]
        before = lax.ppermute(value[rows - REACH :], "tensor", along)
        after = lax.ppermute(value[:REACH], "tensor", [(to, at) for at, to in along])
        long_low = is_long.astype(value.dtype)
        return before * long_low, after * long_low

    value_before, value_after = halo(values)
    values_wide = jnp.concatenate([value_before, values, value_after], axis=0)

    def split(value):
        return value.reshape(value.shape[0], heads, head_size)

    q3, k3, v3 = split(query), split(keys), split(values)
    ql3, kl3 = split(query_land), split(key_land)

    scores_f = jnp.einsum("chd,rhd->hcr", kl3, q3, preferred_element_type=f32) * scale
    top_f = jnp.max(scores_f, axis=1, keepdims=True)
    powers_f = jnp.exp(scores_f - top_f)
    probs_f = powers_f / jnp.sum(powers_f, axis=1, keepdims=True)
    f_low = (probs_f * live_f).astype(bf16)

    invert = partial(landmark_inverse, scale=scale)
    inverse, inverse_back = jax.vjp(invert, ql3.astype(f32), kl3.astype(f32))

    scores_b = jnp.einsum("chd,rhd->hcr", ql3, k3, preferred_element_type=f32) * scale
    top_b = jnp.max(scores_b, axis=2, keepdims=True)
    powers_b = jnp.exp(scores_b - top_b)
    total_b = jnp.sum(powers_b, axis=2, keepdims=True)
    log_own = (top_b + jnp.log(total_b))[:, :, 0]
    carried_own = jnp.einsum(
        "hcr,rhd->chd", (powers_b / total_b).astype(bf16), v3, preferred_element_type=f32
    )
    packed = jnp.concatenate([carried_own.reshape(LAND, width), jnp.transpose(log_own)], axis=1)
    packed_all = over_tensor(packed)
    logs = jnp.transpose(packed_all[:, :, width:], (0, 2, 1))
    log_top = jnp.max(logs, axis=0)
    log_joint = log_top + jnp.log(jnp.sum(jnp.exp(logs - log_top), axis=0))
    shares = jnp.exp(logs - log_joint)
    carried_joint = jnp.einsum(
        "khc,kchd->chd",
        shares,
        packed_all[:, :, :width].reshape(tp_size, LAND, heads, head_size),
        precision=highest,
    )
    carried = jnp.where(is_long, carried_joint, carried_own)
    log_b = jnp.where(is_long, log_joint, log_own)
    probs_b = jnp.exp(scores_b - log_b[:, :, None])
    mixed_low = jnp.einsum("hlm,mhd->lhd", inverse, carried, precision=highest).astype(bf16)
    attention = jnp.einsum("hcr,chd->rhd", f_low, mixed_low, preferred_element_type=f32)

    block = 128
    blocks = rows // block
    reach_wide = block + 2 * REACH

    def windows(wide):
        return jnp.stack(
            [wide[at * block : at * block + reach_wide] for at in range(blocks)]
        ).reshape(blocks, reach_wide, heads, head_size)

    def depthwise(kernel, wide):
        band = banded(kernel.astype(bf16), block)
        return jnp.einsum(
            "hik,bkhd->bihd", band, windows(wide), preferred_element_type=f32
        ).reshape(rows, width)

    conv_part = depthwise(conv_all, values_wide) * live_f
    attended = (attention.reshape(rows, width) + conv_part).astype(bf16)

    summed_one = layer_input.astype(f32) + nn(attended, full_out) + b_out.astype(f32)
    gain_one = norm1_gain.astype(f32)
    normed, unit_one, inv_one = norm_forward(summed_one, gain_one, norm1_bias.astype(f32))
    normed_low = normed.astype(bf16)
    pre_act = nt(normed_low, full_in) + bias_in
    cdf = 0.5 * (1.0 + lax.erf(pre_act * (1.0 / math.sqrt(2.0))))
    hidden_low = (pre_act * cdf).astype(bf16)
    slope = cdf + pre_act * jnp.exp(-0.5 * pre_act * pre_act) * (1.0 / math.sqrt(2.0 * math.pi))
    summed_two = normed + nn(hidden_low, full_back) + b_back.astype(f32)
    gain_two = norm2_gain.astype(f32)
    output, unit_two, inv_two = norm_forward(summed_two, gain_two, norm2_bias.astype(f32))

    out_grad = output_grad.astype(f32)
    grad_two = norm_backward(out_grad, unit_two, inv_two, gain_two)
    grad_two_low = grad_two.astype(bf16)

    back_piece = scatter_near(tn(hidden_low, grad_two_low), down)
    hidden_grad = nt(grad_two_low, full_back)
    pre_grad = (hidden_grad * slope).astype(bf16)
    in_piece = scatter_near(tn(pre_grad, normed_low), up)
    normed_grad = grad_two + nn(pre_grad, full_in)
    grad_one = norm_backward(normed_grad, unit_one, inv_one, gain_one)
    grad_one_low = grad_one.astype(bf16)
    out_piece = scatter_plain(tn(attended, grad_one_low), down)
    attended_grad = nt(grad_one_low, full_out).astype(bf16)

    g3 = split(attended_grad)
    f_grad = (
        jnp.einsum("chd,rhd->hcr", mixed_low, g3, preferred_element_type=f32)
        .astype(bf16)
        .astype(f32)
        * live_f
    )
    score_f_grad = (
        probs_f * (f_grad - jnp.sum(f_grad * probs_f, axis=1, keepdims=True))
    ).astype(bf16)
    query_grad = jnp.einsum("hcr,chd->rhd", score_f_grad, kl3, preferred_element_type=f32) * scale
    key_land_part = (
        jnp.einsum("hcr,rhd->chd", score_f_grad, q3, preferred_element_type=f32) * scale
    )
    mixed_part = jnp.einsum("hcr,rhd->chd", f_low, g3, preferred_element_type=f32).reshape(
        LAND, width
    )
    mixed_grad = (
        jnp.where(is_long, sum_tensor(mixed_part), mixed_part)
        .astype(bf16)
        .astype(f32)
        .reshape(LAND, heads, head_size)
    )
    grad_before, grad_after = halo(attended_grad)
    grads_wide = jnp.concatenate([grad_before, attended_grad, grad_after], axis=0)

    inverse_grad = jnp.einsum("lhd,mhd->hlm", mixed_grad, carried, precision=highest)
    carried_grad = jnp.einsum("hlm,lhd->mhd", inverse, mixed_grad, precision=highest).astype(bf16)
    b_grad = (
        jnp.einsum("chd,rhd->hcr", carried_grad, v3, preferred_element_type=f32)
        .astype(bf16)
        .astype(f32)
    )
    b_low = probs_b.astype(bf16)
    value_grad = jnp.einsum("hcr,chd->rhd", b_low, carried_grad, preferred_element_type=f32)
    along = jnp.transpose(jnp.sum(carried_grad.astype(f32) * carried, axis=2))
    score_b_grad = (probs_b * (b_grad - along[:, :, None])).astype(bf16)
    query_land_part = (
        jnp.einsum("hcr,rhd->chd", score_b_grad, k3, preferred_element_type=f32) * scale
    )
    key_grad = jnp.einsum("hcr,chd->rhd", score_b_grad, ql3, preferred_element_type=f32) * scale
    land_query_grad, land_key_grad = inverse_back(inverse_grad)

    land_part = jnp.concatenate(
        [query_land_part.reshape(LAND, width), key_land_part.reshape(LAND, width)], axis=1
    )
    land_exact = jnp.concatenate(
        [land_query_grad.reshape(LAND, width), land_key_grad.reshape(LAND, width)], axis=1
    )
    own_first = tp_at * share_long
    by_owner = land_part.reshape(tp_size, share_long, 2 * width)
    own_part = lax.dynamic_index_in_dim(by_owner, tp_at, axis=0, keepdims=False)
    for far in range(1, tp_size):
        sent = lax.dynamic_index_in_dim(by_owner, tp_at ^ far, axis=0, keepdims=False)
        own_part = own_part + partner(sent, ("tensor", 0), far)
    land_low_long = (
        own_part + lax.dynamic_slice_in_dim(land_exact, own_first, share_long, axis=0)
    ).astype(bf16)
    land_low_short = (land_part + land_exact).astype(bf16)
    spread = jnp.where(
        is_long, tn(pick_long, land_low_long), tn(pick_short, land_low_short)
    ) * (live_f / per_column)
    query_grad = query_grad.reshape(rows, width) + spread[:, :width]
    key_grad = key_grad.reshape(rows, width) + spread[:, width:]
    value_grad = value_grad.reshape(rows, width) + live_f * depthwise(
        conv_all[:, ::-1], grads_wide
    )
    live_b = live.astype(bf16)
    query_low = query_grad.astype(bf16)
    key_low = key_grad.astype(bf16) * live_b
    value_low = value_grad.astype(bf16)

    outer = jnp.einsum(
        "bihd,bkhd->hik",
        attended_grad.reshape(blocks, block, heads, head_size),
        windows(values_wide),
        preferred_element_type=f32,
    )
    taps = conv_w.shape[1]
    skewed = jnp.pad(outer.reshape(heads, block * reach_wide), ((0, 0), (0, block))).reshape(
        heads, block, reach_wide + 1
    )
    conv_grad = jnp.sum(skewed, axis=1)[:, :taps] * live_f

    q_piece = scatter_plain(tn(query_low, layer_input), up)
    k_piece = scatter_plain(tn(key_low, layer_input), up)
    v_piece = scatter_plain(tn(value_low, layer_input), down)
    input_grad = grad_one + nn(query_low, full_q) + nn(key_low, full_k) + nn(value_low, full_v)

    def sum_rows(value):
        return jnp.sum(value.astype(f32), axis=0)

    vectors = jnp.concatenate(
        [
            sum_rows(grad_one),
            sum_rows(normed_grad * unit_one),
            sum_rows(normed_grad),
            sum_rows(grad_two),
            sum_rows(out_grad * unit_two),
            sum_rows(out_grad),
            sum_rows(query_low),
            sum_rows(value_low),
            sum_rows(pre_grad).reshape(-1, hidden_share)[plain_to_near].reshape(-1),
            jnp.pad(conv_grad.reshape(-1), (0, width - conv_grad.size)),
        ]
    ).reshape(-1, width)
    for step in on_core + up + on_tensor:
        vectors = vectors + partner(vectors, step)

    def own(vector, count):
        return lax.dynamic_slice_in_dim(vector, tp_at * count, count, axis=0)

    w_qkv_grad = jnp.stack(
        [
            jnp.transpose(over_dp(q_piece, up)),
            jnp.transpose(over_dp(k_piece, up)),
            jnp.transpose(over_dp(v_piece, down)),
        ],
        axis=1,
    )
    return (
        output,
        input_grad,
        w_qkv_grad,
        jnp.stack([own(vectors[6], local_width), own(vectors[7], local_width)]),
        over_dp(out_piece, down),
        vectors[0],
        own(vectors[12][: conv_grad.size].reshape(heads, taps), local_heads),
        vectors[1],
        vectors[2],
        jnp.transpose(over_dp(in_piece, up)),
        own(vectors[8:12].reshape(-1), b_in.shape[0]),
        over_dp(back_piece, down),
        vectors[3],
        vectors[4],
        vectors[5],
    )


def solution(mesh):
    placed = (
        P(("dp", "tensor"), None),
        P(None, None, "tensor"),
        P(None, "tensor"),
        P("tensor", None),
        P(),
        P("tensor", None),
        P(),
        P(),
        P(None, "tensor"),
        P("tensor"),
        P("tensor", None),
        P(),
        P(),
        P(),
        P(("dp", "tensor"), None),
        P(),
        P(),
        P(),
    )
    return jax.shard_map(
        partial(on_device, mesh.shape["dp"], mesh.shape["tensor"]),
        mesh=mesh,
        in_specs=placed,
        out_specs=(
            P(("dp", "tensor"), None),
            P(("dp", "tensor"), None),
            P(None, None, "tensor"),
            P(None, "tensor"),
            P("tensor", None),
            P(),
            P("tensor", None),
            P(),
            P(),
            P(None, "tensor"),
            P("tensor"),
            P("tensor", None),
            P(),
            P(),
            P(),
        ),
        check_vma=False,
    )
```

```python
from functools import partial
import math

import jax
import jax.numpy as jnp
import numpy as np
from jax import lax
from jax.sharding import PartitionSpec as P

LAND = 64
NS_STEPS = 6
SHORT = 512
REACH = 16

highest = lax.Precision.HIGHEST
eps = 1e-05
f32 = jnp.float32
bf16 = jnp.bfloat16


def dot(left, right, dims, precision=None):
    return lax.dot_general(
        left, right, (dims, ((), ())), preferred_element_type=f32, precision=precision
    )


def nn(left, right):
    return dot(left, right, ((1,), (0,)))


def nt(left, right):
    return dot(left, right, ((1,), (1,)))


def tn(left, right):
    return dot(left, right, ((0,), (0,)))


def landmark_inverse(query_land, key_land, scale):
    scores = jnp.einsum("lhd,mhd->hlm", query_land, key_land, precision=highest) * scale
    weight = jax.nn.softmax(scores, axis=-1)
    row_top = jnp.max(jnp.sum(weight, axis=-1), axis=-1)
    col_top = jnp.max(jnp.sum(weight, axis=-2), axis=-1)
    inverse = jnp.swapaxes(weight, -1, -2) / (row_top * col_top)[:, None, None]
    identity = jnp.eye(weight.shape[-1], dtype=f32)
    for sweep_index in range(NS_STEPS):
        product = jnp.matmul(weight, inverse, precision=lax.Precision.HIGH)
        factor = 7.0 * identity - product
        factor = 15.0 * identity - jnp.matmul(product, factor, precision=lax.Precision.HIGH)
        factor = 13.0 * identity - jnp.matmul(product, factor, precision=lax.Precision.HIGH)
        inverse = 0.25 * jnp.matmul(inverse, factor, precision=lax.Precision.HIGH)
    return inverse


def normalize(summed, gain, shift):
    centered = summed - jnp.mean(summed, axis=-1, keepdims=True)
    spread = jnp.mean(centered * centered, axis=-1, keepdims=True)
    return centered * lax.rsqrt(spread + eps) * gain + shift


def norm_forward(summed, gain, shift):
    centered = summed - jnp.mean(summed, axis=-1, keepdims=True)
    spread = jnp.mean(centered * centered, axis=-1, keepdims=True)
    inv = lax.rsqrt(spread + eps)
    unit = centered * inv
    return unit * gain + shift, unit, inv


def norm_backward(grad, unit, inv, gain):
    scaled = grad * gain
    first = jnp.mean(scaled, axis=-1, keepdims=True)
    second = jnp.mean(scaled * unit, axis=-1, keepdims=True)
    return inv * (scaled - first - unit * second)


def banded(kernel, block):
    heads, taps = kernel.shape
    wide = block + taps - 1
    padded = jnp.pad(kernel, ((0, 0), (0, wide + 1 - taps)))
    tiled = jnp.tile(padded, (1, block))[:, : block * wide]
    return tiled.reshape(heads, block, wide)


def on_device(
    dp_size,
    tp_size,
    layer_input,
    w_qkv,
    b_qv,
    w_out,
    b_out,
    conv_w,
    norm1_gain,
    norm1_bias,
    w_in,
    b_in,
    w_back,
    b_back,
    norm2_gain,
    norm2_bias,
    output_grad,
    item_length,
    item_group,
    item_offset,
):
    rows, width = layer_input.shape
    local_width = w_qkv.shape[2]
    local_heads = conv_w.shape[0]
    head_size = local_width // local_heads
    heads = local_heads * tp_size
    scale = 1.0 / math.sqrt(head_size)
    dp_at = lax.axis_index("dp")
    tp_at = lax.axis_index("tensor")
    sizes = {"dp": dp_size, "tensor": tp_size}
    places = {"dp": dp_at, "tensor": tp_at}
    dp_bits = dp_size.bit_length() - 1
    tp_bits = tp_size.bit_length() - 1
    on_tensor = [("tensor", bit) for bit in range(tp_bits)]
    on_core = [("dp", 0)]
    up = [("dp", bit) for bit in range(1, dp_bits)]
    down = up[::-1]
    axes = on_core + down + on_tensor[::-1]

    def partner(value, step, distance=None):
        axis, bit = step
        flip = distance if distance is not None else 1 << bit
        return lax.ppermute(value, axis, [(at, at ^ flip) for at in range(sizes[axis])])

    def is_upper(step):
        return (places[step[0]] >> step[1]) & 1

    def joined(value, other, upper, axis):
        if upper is None:
            return jnp.concatenate([value, other], axis=axis)
        first = jnp.where(upper == 1, other, value)
        second = jnp.where(upper == 1, value, other)
        return jnp.concatenate([first, second], axis=axis)

    def gather_steps(mine, steps, order, absolute):
        held = mine.reshape((1,) * len(order) + mine.shape)
        for step in steps:
            other = partner(held, step)
            held = joined(held, other, is_upper(step) if absolute else None, order.index(step))
        return held.reshape((-1,) + mine.shape[1:])

    def own_share(local):
        share = local.shape[0] // dp_size
        return lax.dynamic_slice_in_dim(local, dp_at * share, share, axis=0)

    plain = on_tensor[::-1] + down + on_core

    def gather_plain(local, middle):
        return gather_steps(own_share(local), on_tensor[::-1] + middle + on_core, plain, True)

    def gather_near(local, middle):
        return gather_steps(own_share(local), on_tensor[::-1] + middle + on_core, axes, False)

    def scatter_plain(partial_sum, middle):
        held = partial_sum.reshape((2,) * len(plain) + (-1, partial_sum.shape[1]))
        left = list(plain)
        for step in on_core + middle + on_tensor:
            at = left.index(step)
            upper = is_upper(step)
            sent = lax.dynamic_index_in_dim(held, 1 - upper, axis=at, keepdims=False)
            kept = lax.dynamic_index_in_dim(held, upper, axis=at, keepdims=False)
            held = kept + partner(sent.astype(bf16), step).astype(f32)
            left.remove(step)
        return held

    def scatter_near(partial_sum, middle):
        held = partial_sum.reshape((2,) * len(axes) + (-1, partial_sum.shape[1]))
        left = list(axes)
        for step in on_core + middle + on_tensor:
            at = left.index(step)
            sent = lax.index_in_dim(held, 1, axis=at, keepdims=False)
            kept = lax.index_in_dim(held, 0, axis=at, keepdims=False)
            held = kept + partner(sent.astype(bf16), step).astype(f32)
            left.remove(step)
        return held

    def over_tensor(value):
        parts = [value] + [partner(value, ("tensor", 0), far) for far in range(1, tp_size)]
        for bit in range(tp_bits):
            upper = is_upper(("tensor", bit)) == 1
            parts = [jnp.where(upper, parts[at ^ (1 << bit)], parts[at]) for at in range(tp_size)]
        return jnp.stack(parts)

    def sum_tensor(value):
        parts = [value] + [partner(value, ("tensor", 0), far) for far in range(1, tp_size)]
        while len(parts) > 1:
            parts = [parts[at] + parts[at + 1] for at in range(0, len(parts), 2)]
        return parts[0]

    def over_dp(piece, middle):
        rounded = lax.reduce_precision(piece, 8, 7).astype(bf16)
        return gather_steps(rounded, middle + on_core, down + on_core, True).astype(f32)

    local_qkv = jnp.transpose(w_qkv, (1, 2, 0)).reshape(3 * local_width, width)
    full_q = gather_plain(local_qkv[:local_width], up)
    full_k = gather_plain(local_qkv[local_width : 2 * local_width], up)
    full_v = gather_plain(local_qkv[2 * local_width :], down)
    full_out = gather_plain(w_out, down)
    full_in = gather_near(jnp.transpose(w_in), up)
    full_back = gather_near(w_back, down)
    small = jnp.concatenate(
        [
            b_qv.astype(f32).reshape(2, local_width),
            jnp.pad(conv_w.astype(f32).reshape(1, -1), ((0, 0), (0, local_width - conv_w.size))),
            b_in.astype(f32).reshape(-1, local_width),
        ]
    )
    small_all = over_tensor(small)
    bias_q = small_all[:, 0].reshape(-1)
    bias_v = small_all[:, 1].reshape(-1)
    conv_all = small_all[:, 2, : conv_w.size].reshape(heads, conv_w.shape[1])
    hidden_share = b_in.shape[0] // dp_size
    bias_plain = small_all[:, 3:].reshape(dp_size * tp_size, hidden_share)
    codes = jnp.zeros((), jnp.int32)
    plain_index = np.zeros((1,), np.int32)
    for step in axes:
        weight = (1 << step[1]) * (dp_size if step[0] == "tensor" else 1)
        codes = codes + is_upper(step) * weight
        plain_index = (plain_index[:, None] + np.array([0, weight], np.int32)).reshape(-1)
    near_to_plain = plain_index ^ codes
    plain_to_near = jnp.asarray(np.argsort(plain_index).astype(np.int32))[jnp.arange(dp_size * tp_size) ^ codes]
    bias_in = bias_plain[near_to_plain].reshape(-1)

    first_row = tp_at * rows
    holds = (
        (item_group == dp_at)
        & (item_offset <= first_row)
        & (first_row < item_offset + item_length)
    )
    live = jnp.any(holds)
    size = jnp.sum(jnp.where(holds, item_length, 0))
    is_long = size > SHORT
    live_f = live.astype(f32)
    row_ids = jnp.arange(rows, dtype=jnp.int32)
    land_ids = jnp.arange(LAND, dtype=jnp.int32)
    share_long = LAND // tp_size
    per_short = rows // LAND
    per_long = rows // share_long
    per_column = jnp.where(is_long, per_long, per_short).astype(f32)
    pick_short = ((row_ids // per_short)[None, :] == land_ids[:, None]).astype(bf16)
    pick_long = (
        (row_ids // per_long)[None, :] == jnp.arange(share_long, dtype=jnp.int32)[:, None]
    ).astype(bf16)

    query = (nt(layer_input, full_q) + bias_q).astype(bf16)
    keys = nt(layer_input, full_k).astype(bf16)
    values = (nt(layer_input, full_v) + bias_v).astype(bf16)

    both = jnp.concatenate([query, keys], axis=1)
    land_short = (nn(pick_short, both) / per_short).astype(bf16)
    land_long = (nn(pick_long, both) / per_long).astype(bf16)
    land_all = jnp.where(is_long, over_tensor(land_long).reshape(LAND, 2 * width), land_short)
    query_land = land_all[:, :width]
    key_land = land_all[:, width:]

    def halo(value):
        along = [(at, at + 1) for at in range(tp_size - 1)]
        before = lax.ppermute(value[rows - REACH :], "tensor", along)
        after = lax.ppermute(value[:REACH], "tensor", [(to, at) for at, to in along])
        long_low = is_long.astype(value.dtype)
        return before * long_low, after * long_low

    value_before, value_after = halo(values)
    values_wide = jnp.concatenate([value_before, values, value_after], axis=0)

    def split(value):
        return value.reshape(value.shape[0], heads, head_size)

    q3, k3, v3 = split(query), split(keys), split(values)
    ql3, kl3 = split(query_land), split(key_land)

    scores_f = jnp.einsum("chd,rhd->hcr", kl3, q3, preferred_element_type=f32) * scale
    top_f = jnp.max(scores_f, axis=1, keepdims=True)
    powers_f = jnp.exp(scores_f - top_f)
    probs_f = powers_f / jnp.sum(powers_f, axis=1, keepdims=True)
    f_low = (probs_f * live_f).astype(bf16)

    invert = partial(landmark_inverse, scale=scale)
    inverse, inverse_back = jax.vjp(invert, ql3.astype(f32), kl3.astype(f32))

    scores_b = jnp.einsum("chd,rhd->hcr", ql3, k3, preferred_element_type=f32) * scale
    top_b = jnp.max(scores_b, axis=2, keepdims=True)
    powers_b = jnp.exp(scores_b - top_b)
    total_b = jnp.sum(powers_b, axis=2, keepdims=True)
    log_own = (top_b + jnp.log(total_b))[:, :, 0]
    carried_own = jnp.einsum(
        "hcr,rhd->chd", (powers_b / total_b).astype(bf16), v3, preferred_element_type=f32
    )
    packed = jnp.concatenate([carried_own.reshape(LAND, width), jnp.transpose(log_own)], axis=1)
    packed_all = over_tensor(packed)
    logs = jnp.transpose(packed_all[:, :, width:], (0, 2, 1))
    log_top = jnp.max(logs, axis=0)
    log_joint = log_top + jnp.log(jnp.sum(jnp.exp(logs - log_top), axis=0))
    shares = jnp.exp(logs - log_joint)
    carried_joint = jnp.einsum(
        "khc,kchd->chd",
        shares,
        packed_all[:, :, :width].reshape(tp_size, LAND, heads, head_size),
        precision=highest,
    )
    carried = jnp.where(is_long, carried_joint, carried_own)
    log_b = jnp.where(is_long, log_joint, log_own)
    probs_b = jnp.exp(scores_b - log_b[:, :, None])
    mixed_low = jnp.einsum("hlm,mhd->lhd", inverse, carried, precision=highest).astype(bf16)
    attention = jnp.einsum("hcr,chd->rhd", f_low, mixed_low, preferred_element_type=f32)

    block = 128
    blocks = rows // block
    reach_wide = block + 2 * REACH

    def windows(wide):
        return jnp.stack(
            [wide[at * block : at * block + reach_wide] for at in range(blocks)]
        ).reshape(blocks, reach_wide, heads, head_size)

    def depthwise(kernel, wide):
        band = banded(kernel.astype(bf16), block)
        return jnp.einsum(
            "hik,bkhd->bihd", band, windows(wide), preferred_element_type=f32
        ).reshape(rows, width)

    conv_part = depthwise(conv_all, values_wide) * live_f
    attended = (attention.reshape(rows, width) + conv_part).astype(bf16)

    summed_one = layer_input.astype(f32) + nn(attended, full_out) + b_out.astype(f32)
    gain_one = norm1_gain.astype(f32)
    normed, unit_one, inv_one = norm_forward(summed_one, gain_one, norm1_bias.astype(f32))
    normed_low = normed.astype(bf16)
    pre_act = nt(normed_low, full_in) + bias_in
    cdf = 0.5 * (1.0 + lax.erf(pre_act * (1.0 / math.sqrt(2.0))))
    hidden_low = (pre_act * cdf).astype(bf16)
    slope = cdf + pre_act * jnp.exp(-0.5 * pre_act * pre_act) * (1.0 / math.sqrt(2.0 * math.pi))
    summed_two = normed + nn(hidden_low, full_back) + b_back.astype(f32)
    gain_two = norm2_gain.astype(f32)
    output, unit_two, inv_two = norm_forward(summed_two, gain_two, norm2_bias.astype(f32))

    out_grad = output_grad.astype(f32)
    grad_two = norm_backward(out_grad, unit_two, inv_two, gain_two)
    grad_two_low = grad_two.astype(bf16)

    back_piece = scatter_near(tn(hidden_low, grad_two_low), down)
    hidden_grad = nt(grad_two_low, full_back)
    pre_grad = (hidden_grad * slope).astype(bf16)
    in_piece = scatter_near(tn(pre_grad, normed_low), up)
    normed_grad = grad_two + nn(pre_grad, full_in)
    grad_one = norm_backward(normed_grad, unit_one, inv_one, gain_one)
    grad_one_low = grad_one.astype(bf16)
    out_piece = scatter_plain(tn(attended, grad_one_low), down)
    attended_grad = nt(grad_one_low, full_out).astype(bf16)

    g3 = split(attended_grad)
    f_grad = (
        jnp.einsum("chd,rhd->hcr", mixed_low, g3, preferred_element_type=f32)
        .astype(bf16)
        .astype(f32)
        * live_f
    )
    score_f_grad = (
        probs_f * (f_grad - jnp.sum(f_grad * probs_f, axis=1, keepdims=True))
    ).astype(bf16)
    query_grad = jnp.einsum("hcr,chd->rhd", score_f_grad, kl3, preferred_element_type=f32) * scale
    key_land_part = (
        jnp.einsum("hcr,rhd->chd", score_f_grad, q3, preferred_element_type=f32) * scale
    )
    mixed_part = jnp.einsum("hcr,rhd->chd", f_low, g3, preferred_element_type=f32).reshape(
        LAND, width
    )
    mixed_grad = (
        jnp.where(is_long, sum_tensor(mixed_part), mixed_part)
        .astype(bf16)
        .astype(f32)
        .reshape(LAND, heads, head_size)
    )
    grad_before, grad_after = halo(attended_grad)
    grads_wide = jnp.concatenate([grad_before, attended_grad, grad_after], axis=0)

    inverse_grad = jnp.einsum("lhd,mhd->hlm", mixed_grad, carried, precision=highest)
    carried_grad = jnp.einsum("hlm,lhd->mhd", inverse, mixed_grad, precision=highest).astype(bf16)
    b_grad = (
        jnp.einsum("chd,rhd->hcr", carried_grad, v3, preferred_element_type=f32)
        .astype(bf16)
        .astype(f32)
    )
    b_low = probs_b.astype(bf16)
    value_grad = jnp.einsum("hcr,chd->rhd", b_low, carried_grad, preferred_element_type=f32)
    along = jnp.transpose(jnp.sum(carried_grad.astype(f32) * carried, axis=2))
    score_b_grad = (probs_b * (b_grad - along[:, :, None])).astype(bf16)
    query_land_part = (
        jnp.einsum("hcr,rhd->chd", score_b_grad, k3, preferred_element_type=f32) * scale
    )
    key_grad = jnp.einsum("hcr,chd->rhd", score_b_grad, ql3, preferred_element_type=f32) * scale
    land_query_grad, land_key_grad = inverse_back(inverse_grad)

    land_part = jnp.concatenate(
        [query_land_part.reshape(LAND, width), key_land_part.reshape(LAND, width)], axis=1
    )
    land_exact = jnp.concatenate(
        [land_query_grad.reshape(LAND, width), land_key_grad.reshape(LAND, width)], axis=1
    )
    own_first = tp_at * share_long
    by_owner = land_part.reshape(tp_size, share_long, 2 * width)
    own_part = lax.dynamic_index_in_dim(by_owner, tp_at, axis=0, keepdims=False)
    for far in range(1, tp_size):
        sent = lax.dynamic_index_in_dim(by_owner, tp_at ^ far, axis=0, keepdims=False)
        own_part = own_part + partner(sent, ("tensor", 0), far)
    land_low_long = (
        own_part + lax.dynamic_slice_in_dim(land_exact, own_first, share_long, axis=0)
    ).astype(bf16)
    land_low_short = (land_part + land_exact).astype(bf16)
    spread = jnp.where(
        is_long, tn(pick_long, land_low_long), tn(pick_short, land_low_short)
    ) * (live_f / per_column)
    query_grad = query_grad.reshape(rows, width) + spread[:, :width]
    key_grad = key_grad.reshape(rows, width) + spread[:, width:]
    value_grad = value_grad.reshape(rows, width) + live_f * depthwise(
        conv_all[:, ::-1], grads_wide
    )
    live_b = live.astype(bf16)
    query_low = query_grad.astype(bf16)
    key_low = key_grad.astype(bf16) * live_b
    value_low = value_grad.astype(bf16)

    outer = jnp.einsum(
        "bihd,bkhd->hik",
        attended_grad.reshape(blocks, block, heads, head_size),
        windows(values_wide),
        preferred_element_type=f32,
    )
    taps = conv_w.shape[1]
    skewed = jnp.pad(outer.reshape(heads, block * reach_wide), ((0, 0), (0, block))).reshape(
        heads, block, reach_wide + 1
    )
    conv_grad = jnp.sum(skewed, axis=1)[:, :taps] * live_f

    q_piece = scatter_plain(tn(query_low, layer_input), up)
    k_piece = scatter_plain(tn(key_low, layer_input), up)
    v_piece = scatter_plain(tn(value_low, layer_input), down)
    input_grad = grad_one + nn(query_low, full_q) + nn(key_low, full_k) + nn(value_low, full_v)

    def sum_rows(value):
        return jnp.sum(value.astype(f32), axis=0)

    vectors = jnp.concatenate(
        [
            sum_rows(grad_one),
            sum_rows(normed_grad * unit_one),
            sum_rows(normed_grad),
            sum_rows(grad_two),
            sum_rows(out_grad * unit_two),
            sum_rows(out_grad),
            sum_rows(query_low),
            sum_rows(value_low),
            sum_rows(pre_grad).reshape(-1, hidden_share)[plain_to_near].reshape(-1),
            jnp.pad(conv_grad.reshape(-1), (0, width - conv_grad.size)),
        ]
    ).reshape(-1, width)
    for step in on_core + up + on_tensor:
        vectors = vectors + partner(vectors, step)

    def own(vector, count):
        return lax.dynamic_slice_in_dim(vector, tp_at * count, count, axis=0)

    w_qkv_grad = jnp.stack(
        [
            jnp.transpose(over_dp(q_piece, up)),
            jnp.transpose(over_dp(k_piece, up)),
            jnp.transpose(over_dp(v_piece, down)),
        ],
        axis=1,
    )
    return (
        output,
        input_grad,
        w_qkv_grad,
        jnp.stack([own(vectors[6], local_width), own(vectors[7], local_width)]),
        over_dp(out_piece, down),
        vectors[0],
        own(vectors[12][: conv_grad.size].reshape(heads, taps), local_heads),
        vectors[1],
        vectors[2],
        jnp.transpose(over_dp(in_piece, up)),
        own(vectors[8:12].reshape(-1), b_in.shape[0]),
        over_dp(back_piece, down),
        vectors[3],
        vectors[4],
        vectors[5],
    )


def solution(mesh):
    placed = (
        P(("dp", "tensor"), None),
        P(None, None, "tensor"),
        P(None, "tensor"),
        P("tensor", None),
        P(),
        P("tensor", None),
        P(),
        P(),
        P(None, "tensor"),
        P("tensor"),
        P("tensor", None),
        P(),
        P(),
        P(),
        P(("dp", "tensor"), None),
        P(),
        P(),
        P(),
    )
    return jax.shard_map(
        partial(on_device, mesh.shape["dp"], mesh.shape["tensor"]),
        mesh=mesh,
        in_specs=placed,
        out_specs=(
            P(("dp", "tensor"), None),
            P(("dp", "tensor"), None),
            P(None, None, "tensor"),
            P(None, "tensor"),
            P("tensor", None),
            P(),
            P("tensor", None),
            P(),
            P(),
            P(None, "tensor"),
            P("tensor"),
            P("tensor", None),
            P(),
            P(),
            P(),
        ),
        check_vma=False,
    )
```
